32 devices in a mesh: wide: 8 (over y, x, core), narrow: 4 (over z).
Axes of the slice: x: 2, y: 2, z: 4, core: 2. Of those that a mesh axis runs over, the one named last changes fastest.
Arguments:
- tokens: bfloat16 [8192, 1536], P(('wide', 'narrow')), may hold values from -6 to 6
- cotangent: bfloat16 [8192, 1536], P(('wide', 'narrow')), may hold values from -6 to 6
- lengths: int32 [8], replicated, may hold values from 1 to 2048, 8192 in all
- gain_attn: float32 [2, 1536], replicated, may hold values from 0.5 to 1.5
- w_query: bfloat16 [2, 1536, 1536], P(None, None, 'narrow'), may hold values from -0.15625 to 0.15625
- w_key: bfloat16 [2, 1536, 768], P(None, None, 'narrow'), may hold values from -0.15625 to 0.15625
- w_value: bfloat16 [2, 1536, 768], P(None, None, 'narrow'), may hold values from -0.15625 to 0.15625
- w_out: bfloat16 [2, 1536, 1536], P(None, 'narrow'), may hold values from -3 to 3
- gain_mlp: float32 [2, 1536], replicated, may hold values from 0.5 to 1.5
- w_gate: bfloat16 [2, 1536, 4096], P(None, None, 'narrow'), may hold values from -0.15625 to 0.15625
- w_up: bfloat16 [2, 1536, 4096], P(None, None, 'narrow'), may hold values from -0.15625 to 0.15625
- w_down: bfloat16 [2, 4096, 1536], P(None, 'narrow'), may hold values from -0.09375 to 0.09375
Outputs:
- output: float32 [8192, 1536], P(('wide', 'narrow'))
- input_grad: float32 [8192, 1536], P(('wide', 'narrow'))
- grad_gain_attn: float32 [2, 1536], replicated
- grad_w_query: float32 [2, 1536, 1536], P(None, None, 'narrow')
- grad_w_key: float32 [2, 1536, 768], P(None, None, 'narrow')
- grad_w_value: float32 [2, 1536, 768], P(None, None, 'narrow')
- grad_w_out: float32 [2, 1536, 1536], P(None, 'narrow')
- grad_gain_mlp: float32 [2, 1536], replicated
- grad_w_gate: float32 [2, 1536, 4096], P(None, None, 'narrow')
- grad_w_up: float32 [2, 1536, 4096], P(None, None, 'narrow')
- grad_w_down: float32 [2, 4096, 1536], P(None, 'narrow')
The draws below stay inside these ranges and needn't reach their ends.
Inputs may be any that keep to these rules, and one draw needn't show every extreme that they name: The lengths sum to 8192; the largest is exactly 2048.
All inputs are finite; a program needn't handle non-finite values.
Results may differ from the reference program's by a relative error of at most 0.03.
Values may be sent and summed in bfloat16 or wider, within the bound.
No kernel may reach another device: no remote copies, remote signals or barrier semaphores. Data moves between devices by JAX's collectives and lax.ppermute only.
A program may use at most 256 MiB of HBM per device.

```python
import math
import jax
import jax.numpy as jnp
import numpy as np
from jax import lax

D = 1536
FF = 4096
HEADS = 16
KV_HEADS = 8
HD = 96
LAYERS = 2
SEQS = 8
TOKENS = 8192
MOST = 2048


def block_levels(key, shape, split, smallest, high):
    def one(axis_at, shards_of):
        steps = jax.random.uniform(jax.random.fold_in(jax.random.fold_in(key, 6), axis_at), (shards_of,), jnp.float32, smallest / len(split), high / len(split))
        return jnp.repeat(jnp.exp(steps), shape[axis_at] // shards_of).reshape((-1,) + (1,) * (len(shape) - axis_at - 1))

    level = one(*split[0])
    for cut in split[1:]:
        level = level * one(*cut)
    return level


def length_profile(number_of, total, reach, skew):
    portions = [(1 << 20) // math.isqrt(standing ** skew) + 1 for standing in range(2, number_of + 1)]
    surplus, holding = total - reach - (number_of - 1), [1] * (number_of - 1)
    while surplus > 0:
        free = [i for i in range(number_of - 1) if holding[i] < reach]
        whole, remaining = sum([portions[i] for i in free]), surplus
        for i in free:
            more = min(reach - holding[i], max(1, remaining * portions[i] // whole), surplus)
            holding[i] = holding[i] + more
            surplus = surplus - more
    return np.array([reach] + holding)


def ragged(own_key, count, total, limit, skew):
    if count == 2:
        one = jax.random.randint(own_key, (), max(1, total - limit), min(limit, total - 1) + 1)
        return jnp.stack([one, total - one])
    tallies = jnp.asarray(length_profile(count, total, limit, skew), jnp.int32)
    pairs = (count - 1) // 2
    donor, taker = tallies[1:1 + 2 * pairs:2], tallies[2:2 + 2 * pairs:2]
    slack = jnp.minimum(donor - 1, limit - taker)
    shifted = jax.random.randint(jax.random.fold_in(own_key, 1), (pairs,), 0, 1 << 20) % (slack + 1)
    tallies = tallies.at[1:1 + 2 * pairs:2].set(donor - shifted).at[2:2 + 2 * pairs:2].set(taker + shifted)
    return tallies[jax.random.permutation(jax.random.fold_in(own_key, 2), count)]


def centred(rng, shape, spread, bound, cuts=(), held_as=jnp.bfloat16):
    drawn = jax.random.normal(rng, shape, jnp.float32) * spread
    if len(cuts) > 0:
        drawn = block_levels(rng, shape, cuts, -0.22, 0.18) * drawn
    return jnp.clip(drawn, min=-bound, max=bound).astype(held_as)


def setup_inputs(seed: int = 0) -> dict:
    seeds = jax.random.split(jax.random.key(seed), 13)
    return {
        "tokens": centred(seeds[0], (TOKENS, D), 1.0, 6.0, ((0, 32),)),
        "cotangent": centred(seeds[1], (TOKENS, D), 1.0, 6.0, ((0, 32),)),
        "lengths": ragged(seeds[2], SEQS, TOKENS, MOST, 2).astype(jnp.int32),
        "gain_attn": jnp.clip(1.0 + 0.1 * jax.random.normal(seeds[3], (LAYERS, D), jnp.float32), 0.5, 1.5),
        "w_query": centred(seeds[4], (LAYERS, D, HEADS * HD), D ** -0.5, 0.15625, ((2, 4),)),
        "w_key": centred(seeds[5], (LAYERS, D, KV_HEADS * HD), D ** -0.5, 0.15625, ((2, 4),)),
        "w_value": centred(seeds[6], (LAYERS, D, KV_HEADS * HD), D ** -0.5, 0.15625, ((2, 4),)),
        "w_out": centred(seeds[7], (LAYERS, HEADS * HD, D), 4 ** -0.5, 3.0, ((1, 4),)),
        "gain_mlp": jnp.clip(1.0 + 0.1 * jax.random.normal(seeds[8], (LAYERS, D), jnp.float32), 0.5, 1.5),
        "w_gate": centred(seeds[9], (LAYERS, D, FF), D ** -0.5, 0.15625, ((2, 4),)),
        "w_up": centred(seeds[10], (LAYERS, D, FF), D ** -0.5, 0.15625, ((2, 4),)),
        "w_down": centred(seeds[11], (LAYERS, FF, D), FF ** -0.5, 0.09375, ((1, 4),)),
    }


EPSILON = 1e-05
ROPE_BASE = 100000.0
MASKED = -1e+30

@jax.custom_vjp
def low(v):
    return lax.optimization_barrier(v.astype(jnp.bfloat16)).astype(jnp.float32)

@jax.custom_vjp
def low_back(v):
    return v

def low_keep(v):
    return (low(v), None)

def low_pass(kept, grad):
    return (grad,)

def back_keep(v):
    return (v, None)

def back_low(kept, grad):
    return (low(grad),)
low.defvjp(low_keep, low_pass)
low_back.defvjp(back_keep, back_low)

def product(left, right):
    return jnp.dot(left, right, precision=lax.Precision.HIGHEST)

def rms_scaled(residual, gain):
    return residual * lax.rsqrt(lax.optimization_barrier(jnp.mean(residual * residual, axis=-1, keepdims=True)) + EPSILON) * gain

def rotary(values, position, sign):
    half_dim = values.shape[-1] // 2
    frequency = jnp.power(ROPE_BASE, -jnp.arange(half_dim, dtype=jnp.float32) / half_dim)
    angles = position.astype(jnp.float32)[:, None] * frequency[None, :]
    cosine = jnp.cos(angles)[:, None, :]
    sine_term = sign * jnp.sin(angles)[:, None, :]
    first_half = values[..., :half_dim]
    second = values[..., half_dim:]
    return jnp.concatenate([first_half * cosine - second * sine_term, second * cosine + first_half * sine_term], axis=-1)

def locate_tokens(token_index, lengths):
    seq_ends = jnp.cumsum(lengths).astype(jnp.int32)
    seq_starts = (seq_ends - lengths).astype(jnp.int32)
    segment = lax.optimization_barrier(jnp.sum((token_index[:, None] >= seq_ends[None, :]).astype(jnp.int32), axis=1)).astype(jnp.int32)
    picked = segment[:, None] == jnp.arange(lengths.shape[0], dtype=jnp.int32)[None, :]
    seq_begin = lax.optimization_barrier(jnp.sum(jnp.where(picked, seq_starts[None, :], 0), axis=1)).astype(jnp.int32)
    return (segment, (token_index - seq_begin).astype(jnp.int32))

def attention(queries, key_rows, value_rows, segment):
    block_size = math.gcd(TOKENS, 512)
    block_count = TOKENS // block_size
    token_index = jnp.arange(TOKENS, dtype=jnp.int32)
    grouped = queries.reshape(block_count, block_size, KV_HEADS, HEADS // KV_HEADS, HD)

    def one_block(block_item):
        query_block, query_index, query_segment = block_item
        scores = jnp.einsum('qkgd,tkd->kgqt', query_block, key_rows, precision=lax.Precision.HIGHEST) * (1.0 / math.sqrt(HD))
        scores = low_back(scores)
        allowed = (segment[None, :] == query_segment[:, None]) & (token_index[None, :] <= query_index[:, None])
        scores = jnp.where(allowed, scores, MASKED)
        largest = lax.optimization_barrier(jnp.max(scores, axis=-1, keepdims=True))
        weights = jnp.exp(scores - largest)
        probabilities = weights / lax.optimization_barrier(jnp.sum(weights, axis=-1, keepdims=True))
        return jnp.einsum('kgqt,tkd->qkgd', low(probabilities), value_rows, precision=lax.Precision.HIGHEST)
    result = lax.map(jax.checkpoint(one_block), (grouped, token_index.reshape(block_count, block_size), segment.reshape(block_count, block_size)))
    return result.reshape(TOKENS, HEADS * HD)

def layer(residual, params, segment, position):
    gain_first, query_proj, key_proj, value_proj, out_proj, gain_second, gate_proj, up_proj, down_proj = params
    normed_first = low(rms_scaled(residual, gain_first))
    queries = low(rotary(low_back(product(normed_first, query_proj)).reshape(TOKENS, HEADS, HD), position, 1.0))
    key_rows = low(rotary(low_back(product(normed_first, key_proj)).reshape(TOKENS, KV_HEADS, HD), position, 1.0))
    value_rows = low(low_back(product(normed_first, value_proj))).reshape(TOKENS, KV_HEADS, HD)
    attended = attention(queries, key_rows, value_rows, segment)
    mixed = low(low_back(attended))
    middle = residual + low_back(product(mixed, out_proj))
    normed_second = low(rms_scaled(middle, gain_second))
    gate_value = low_back(product(normed_second, gate_proj))
    up_value = low_back(product(normed_second, up_proj))
    active = low(jax.nn.silu(gate_value) * up_value)
    return middle + low_back(product(active, down_proj))

def reference(tokens, cotangent, lengths, gain_attn, w_query, w_key, w_value, w_out, gain_mlp, w_gate, w_up, w_down):
    segment, position = locate_tokens(jnp.arange(TOKENS, dtype=jnp.int32), lengths)
    params = tuple((member.astype(jnp.float32) for member in (gain_attn, w_query, w_key, w_value, w_out, gain_mlp, w_gate, w_up, w_down)))

    def forward(start_rows, weights):
        residual = start_rows
        for layer_index in range(LAYERS):
            residual = layer(residual, tuple((member[layer_index] for member in weights)), segment, position)
        return residual
    result, pullback = jax.vjp(forward, tokens.astype(jnp.float32), params)
    tokens_grad, weight_grads = pullback(cotangent.astype(jnp.float32))
    return (result, tokens_grad, weight_grads[0], weight_grads[1], weight_grads[2], weight_grads[3], weight_grads[4], weight_grads[5], weight_grads[6], weight_grads[7], weight_grads[8])
```

```python
import math

import jax
import jax.numpy as jnp
from jax import lax
from jax.experimental import pallas as pl
from jax.experimental.pallas import tpu as pltpu
from jax.sharding import Mesh
from jax.sharding import PartitionSpec as P

HD = 96
LAYERS = 2
EPSILON = 1e-05
ROPE_BASE = 100000.0
MASKED = -1e30
BLOCK_Q = 256
BLOCK_K = 512
SCALE = 1.0 / math.sqrt(HD)
LOG2_SCALE = math.log2(math.e) * SCALE
BF16 = jnp.bfloat16
F32 = jnp.float32

ALL = ("col", "core", "half", "q")


def side_by_side(ref):
    return jnp.concatenate([ref[h] for h in range(ref.shape[0])], axis=-1)


def masked_offsets(bounds_ref, low_ref, high_ref, q_blocks, group):
    low_q = jnp.concatenate([low_ref[...]] * group, axis=-1)
    span_q = jnp.concatenate([high_ref[...]] * group, axis=-1) - low_q
    inner, outer = (bounds_ref[2 * q_blocks], bounds_ref[2 * q_blocks + 1])
    row = lax.broadcasted_iota(jnp.int32, (BLOCK_K, low_q.shape[1]), 0) ^ inner
    return (low_q, span_q, row, outer)


def flash_forward(bounds, queries, pieces, low, high):
    heads, dim, rows = queries.shape
    kv_count, piece_rows = (pieces[0].shape[1], pieces[0].shape[3])
    keys = piece_rows * len(pieces)
    group = heads // kv_count
    q_blocks = rows // BLOCK_Q
    width = group * BLOCK_Q
    count = len(pieces)

    def kernel(bounds_ref, q_ref, low_ref, high_ref, *refs):
        piece_refs = refs[:count]
        out_ref, mixed_ref, lse_ref, k_rows, values = refs[count:]
        i = pl.program_id(1)

        @pl.when(i == 0)
        def _():
            for b in range(count):
                cut = slice(b * piece_rows, (b + 1) * piece_rows)
                k_rows[cut, :] = piece_refs[b][0, 0].T
                values[:, cut] = piece_refs[b][1, 0]

        q = side_by_side(q_ref)
        low_q, span_q, row, outer = masked_offsets(bounds_ref, low_ref, high_ref, q_blocks, group)

        def step(b, carry):
            top, total, accum = carry
            at = pl.multiple_of((b * BLOCK_K) ^ outer, BLOCK_K)
            scores = jnp.dot(k_rows[pl.ds(at, BLOCK_K), :], q, preferred_element_type=F32) * LOG2_SCALE
            offset = row + (b * BLOCK_K - low_q)
            scores = jnp.where((offset >= 0) & (offset <= span_q), scores, MASKED)
            new_top = jnp.maximum(top, jnp.max(scores, axis=0, keepdims=True))
            probs = jnp.exp2(scores - new_top)
            fade = jnp.exp2(top - new_top)
            total = total * fade + jnp.sum(probs, axis=0, keepdims=True)
            accum = accum * fade + jnp.dot(
                values[:, pl.ds(at, BLOCK_K)], probs.astype(BF16), preferred_element_type=F32
            )
            return (new_top, total, accum)

        start = (
            jnp.full((1, width), MASKED, F32),
            jnp.zeros((1, width), F32),
            jnp.zeros((dim, width), F32),
        )
        top, total, accum = lax.fori_loop(bounds_ref[2 * i], bounds_ref[2 * i + 1], step, start)
        out = accum / total
        lse = top + jnp.log2(total)
        for h in range(group):
            cut = slice(h * BLOCK_Q, (h + 1) * BLOCK_Q)
            out_ref[h] = out[:, cut]
            mixed_ref[h] = out[:, cut].astype(BF16)
            lse_ref[h] = lse[:, cut]

    q_spec = pl.BlockSpec((group, dim, BLOCK_Q), lambda j, i, b: (j, 0, i))
    vector = pl.BlockSpec((1, BLOCK_Q), lambda j, i, b: (0, i))
    piece = pl.BlockSpec((2, 1, dim, piece_rows), lambda j, i, b: (0, j, 0, 0))
    return pl.pallas_call(
        kernel,
        grid_spec=pltpu.PrefetchScalarGridSpec(
            num_scalar_prefetch=1,
            grid=(kv_count, q_blocks),
            in_specs=[q_spec, vector, vector] + [piece] * count,
            out_specs=[q_spec, q_spec, pl.BlockSpec((group, 1, BLOCK_Q), lambda j, i, b: (j, 0, i))],
            scratch_shapes=[pltpu.VMEM((keys, dim), BF16), pltpu.VMEM((dim, keys), BF16)],
        ),
        out_shape=[
            jax.ShapeDtypeStruct((heads, dim, rows), F32),
            jax.ShapeDtypeStruct((heads, dim, rows), BF16),
            jax.ShapeDtypeStruct((heads, 1, rows), F32),
        ],
        compiler_params=pltpu.CompilerParams(vmem_limit_bytes=40 << 20),
        cost_estimate=pl.CostEstimate(
            flops=4 * heads * rows * keys * dim, bytes_accessed=6 << 20, transcendentals=heads * rows * keys
        ),
        name="flash_forward",
    )(bounds, queries, low, high, *pieces)


def flash_backward(bounds, queries, pieces, low, high, lse, out, out_grad, own_count):
    heads, dim, rows = queries.shape
    kv_count, piece_rows = (pieces[0].shape[1], pieces[0].shape[3])
    keys = piece_rows * len(pieces)
    group = heads // kv_count
    q_blocks = rows // BLOCK_Q
    width = group * BLOCK_Q
    count = len(pieces)

    def kernel(bounds_ref, q_ref, low_ref, high_ref, lse_ref, out_ref, g_ref, *refs):
        piece_refs = refs[:count]
        dq_ref = refs[count]
        grad_refs = refs[count + 1 : 2 * count + 1]
        k_rows, v_rows, k_lanes, dk_rows, dv_rows = refs[2 * count + 1 :]
        i = pl.program_id(1)

        @pl.when(i == 0)
        def _():
            for b in range(count):
                cut = slice(b * piece_rows, (b + 1) * piece_rows)
                k_rows[cut, :] = piece_refs[b][0, 0].T
                v_rows[cut, :] = piece_refs[b][1, 0].T
                k_lanes[:, cut] = piece_refs[b][0, 0]
            dk_rows[...] = jnp.zeros_like(dk_rows)
            dv_rows[...] = jnp.zeros_like(dv_rows)

        q, g = (side_by_side(q_ref), side_by_side(g_ref))
        q_rows, g_rows = (q.T, g.T)
        delta = jnp.sum(g.astype(F32) * side_by_side(out_ref), axis=0, keepdims=True)
        lse_q = side_by_side(lse_ref)
        low_q, span_q, row, outer = masked_offsets(bounds_ref, low_ref, high_ref, q_blocks, group)

        def step(b, dq):
            cut = pl.ds(pl.multiple_of((b * BLOCK_K) ^ outer, BLOCK_K), BLOCK_K)
            scores = jnp.dot(k_rows[cut, :], q, preferred_element_type=F32) * LOG2_SCALE
            offset = row + (b * BLOCK_K - low_q)
            probs = jnp.exp2(jnp.where((offset >= 0) & (offset <= span_q), scores - lse_q, MASKED))
            prob_grad = jnp.dot(v_rows[cut, :], g, preferred_element_type=F32)
            score_grad = (probs * (prob_grad - delta)).astype(BF16)
            dv_rows[cut, :] += jnp.dot(probs.astype(BF16), g_rows, preferred_element_type=F32)
            dk_rows[cut, :] += jnp.dot(score_grad, q_rows, preferred_element_type=F32)
            return dq + jnp.dot(k_lanes[:, cut], score_grad, preferred_element_type=F32)

        start = jnp.zeros((dim, width), F32)
        dq = lax.fori_loop(bounds_ref[2 * i], bounds_ref[2 * i + 1], step, start) * SCALE
        for h in range(group):
            dq_ref[h] = dq[:, h * BLOCK_Q : (h + 1) * BLOCK_Q]

        @pl.when(i == q_blocks - 1)
        def _():
            for b in range(count):
                cut = slice(b * piece_rows, (b + 1) * piece_rows)
                grad_refs[b][0, 0] = (dk_rows[cut, :].T * SCALE).astype(grad_refs[b].dtype)
                grad_refs[b][1, 0] = dv_rows[cut, :].T.astype(grad_refs[b].dtype)

    q_spec = pl.BlockSpec((group, dim, BLOCK_Q), lambda j, i, b: (j, 0, i))
    vector = pl.BlockSpec((1, BLOCK_Q), lambda j, i, b: (0, i))
    piece = pl.BlockSpec((2, 1, dim, piece_rows), lambda j, i, b: (0, j, 0, 0))
    types = [BF16] * (count - own_count) + [F32] * own_count
    return pl.pallas_call(
        kernel,
        grid_spec=pltpu.PrefetchScalarGridSpec(
            num_scalar_prefetch=1,
            grid=(kv_count, q_blocks),
            in_specs=[q_spec, vector, vector, pl.BlockSpec((group, 1, BLOCK_Q), lambda j, i, b: (j, 0, i))]
            + [q_spec] * 2
            + [piece] * count,
            out_specs=[q_spec] + [piece] * count,
            scratch_shapes=[
                pltpu.VMEM((keys, dim), BF16),
                pltpu.VMEM((keys, dim), BF16),
                pltpu.VMEM((dim, keys), BF16),
                pltpu.VMEM((keys, dim), F32),
                pltpu.VMEM((keys, dim), F32),
            ],
        ),
        out_shape=[jax.ShapeDtypeStruct((heads, dim, rows), F32)]
        + [jax.ShapeDtypeStruct((2, kv_count, dim, piece_rows), t) for t in types],
        compiler_params=pltpu.CompilerParams(vmem_limit_bytes=48 << 20),
        cost_estimate=pl.CostEstimate(
            flops=10 * heads * rows * keys * dim, bytes_accessed=14 << 20, transcendentals=heads * rows * keys
        ),
        name="flash_backward",
    )(bounds, queries, low, high, lse, out, out_grad, *pieces)


def flip_core(block):
    return lax.ppermute(block, "core", [(0, 1), (1, 0)])


def flip_q(block, bit):
    return lax.ppermute(block, "q", [(i, i ^ bit) for i in range(lax.axis_size("q"))])


def q_bits():
    bit, bits = (1, [])
    while bit < lax.axis_size("q"):
        bits.append(bit)
        bit *= 2
    return bits


def gather_rows(own):
    held = [own]
    for bit in q_bits():
        held = held + [flip_q(block, bit) for block in held]
    return [jnp.concatenate([block, flip_core(block)]) for block in held]


def scatter_sum(parts):
    rows = parts[0].shape[0] // 2
    sums = [part[:rows] + flip_core(part[rows:].astype(BF16)).astype(F32) for part in parts]
    for bit in reversed(q_bits()):
        sums = [sums[i] + flip_q(sums[i ^ bit].astype(BF16), bit).astype(F32) for i in range(bit)]
    return sums[0]


def token_route(back):
    q_size = lax.axis_size("q")

    def index(core, half, q):
        return (core * 2 + half) * q_size + q

    pairs = []
    for core in range(2):
        for half in range(2):
            for q in range(q_size):
                rank = 2 * q + core
                pairs.append((index(half, rank // q_size, rank % q_size), index(core, half, q)))
    return [(b, a) for a, b in pairs] if back else pairs


def move_tokens(rows, back=False):
    return lax.ppermute(rows, ("core", "half", "q"), token_route(back))


def shifted(block, distance):
    count = 2 * lax.axis_size("col")
    route = [(i - distance, i) for i in range(count) if 0 <= i - distance < count]
    return lax.ppermute(block, ("col", "half"), route)


def fetch_weight(own):
    core, half = (lax.axis_index("core"), lax.axis_index("half"))
    rows = own.shape[0] // (2 * lax.axis_size("col"))
    at = (lax.axis_index("col") * 2 + core) * rows
    piece = lax.dynamic_slice_in_dim(own, at, rows, 0)
    piece = lax.ppermute(piece, "half", [(0, 1), (1, 0)])
    other = lax.all_gather(piece, ("col", "core"), axis=0, tiled=True)
    return jnp.where(core == half, own, other)


def reduce_weight_grad(partial_grad):
    half = lax.axis_index("half")
    part = lax.psum_scatter(partial_grad.astype(BF16), "col", scatter_dimension=0, tiled=True)
    part = part.reshape(2, part.shape[0] // 2, part.shape[1])
    kept = lax.dynamic_index_in_dim(part, half, 0, keepdims=False)
    other = lax.dynamic_index_in_dim(part, 1 - half, 0, keepdims=False)
    places = [(core, half) for core in range(2) for half in range(2)]
    kept = lax.ppermute(kept, ("core", "half"), [(c * 2 + h, h * 2 + c) for c, h in places])
    other = lax.ppermute(other, ("core", "half"), [(c * 2 + h, (1 - h) * 2 + c) for c, h in places])
    summed = (kept.astype(F32) + other.astype(F32)).astype(BF16)
    return lax.all_gather(summed, ("col", "core"), axis=0, tiled=True).astype(F32)


def rms_scaled(residual, gain):
    return residual * lax.rsqrt(jnp.mean(residual * residual, axis=-1, keepdims=True) + EPSILON) * gain


def dot(left, right, left_dim, right_dim):
    return lax.dot_general(left, right, (((left_dim,), (right_dim,)), ((), ())), preferred_element_type=F32)


def rotary(values, cosine, sine):
    values = values.reshape(-1, 2, HD // 2, values.shape[-1])
    first, second = (values[:, 0], values[:, 1])
    turned = jnp.stack([first * cosine - second * sine, second * cosine + first * sine], axis=1)
    return turned.reshape(-1, HD, values.shape[-1])


def forward_layer(residual, weights, context):
    gain_first, qkv_proj, out_proj, gain_second, gate_up_proj, down_proj = weights
    bounds, low, high, cosine, sine, reach = context
    q_width, kv_width = (out_proj.shape[0], (qkv_proj.shape[1] - out_proj.shape[0]) // 2)
    normed_first = gather_rows(rms_scaled(residual, gain_first).astype(BF16))
    chip_rows = normed_first[0].shape[0]
    query_parts, own_pieces = ([], [])
    for index, rows in enumerate(normed_first):
        cut = slice(index * chip_rows, (index + 1) * chip_rows)
        qkv = dot(qkv_proj, rows, 0, 1)
        turned = rotary(qkv[: q_width + kv_width], cosine[:, cut], sine[:, cut]).astype(BF16)
        values = qkv[q_width + kv_width :].astype(BF16).reshape(-1, HD, chip_rows)
        query_parts.append(turned[: q_width // HD])
        own_pieces.append(jnp.stack([turned[q_width // HD :], values]))
    pieces = []
    for distance in range(reach, 0, -1):
        pieces += [shifted(piece, distance) for piece in own_pieces]
    pieces += own_pieces
    queries = jnp.concatenate(query_parts, axis=-1)
    attended, mixed, lse = flash_forward(bounds, queries, pieces, low, high)
    mixed = mixed.reshape(q_width, -1)
    parts = [
        dot(mixed[:, i * chip_rows : (i + 1) * chip_rows], out_proj, 0, 0) for i in range(len(normed_first))
    ]
    middle = residual + scatter_sum(parts)
    normed_second = gather_rows(rms_scaled(middle, gain_second).astype(BF16))
    gates, actives, parts = ([], [], [])
    for rows in normed_second:
        gate_up = dot(rows, gate_up_proj, 1, 0)
        gate, up = jnp.split(gate_up, 2, axis=1)
        active = (jax.nn.silu(gate) * up).astype(BF16)
        gates.append((gate, up))
        actives.append(active)
        parts.append(dot(active, down_proj, 1, 0))
    result = middle + scatter_sum(parts)
    saved = (residual, normed_first, queries, pieces, attended, mixed, lse, middle, normed_second, gates, actives)
    return (result, saved)


def backward_layer(gradient, weights, saved, context):
    gain_first, qkv_proj, out_proj, gain_second, gate_up_proj, down_proj = weights
    bounds, low, high, cosine, sine, reach = context
    residual, normed_first, queries, pieces, attended, mixed, lse, middle, normed_second, gates, actives = saved
    chip_rows = normed_first[0].shape[0]
    chips = len(normed_first)
    branch_grads = gather_rows(gradient.astype(BF16))
    gate_up_grads, parts = ([], [])
    for rows, (gate, up) in zip(branch_grads, gates):
        active_grad = dot(rows, down_proj, 1, 1)
        sigmoid_gate = jax.nn.sigmoid(gate)
        gate_grad = (active_grad * up * sigmoid_gate * (1.0 + gate * (1.0 - sigmoid_gate))).astype(BF16)
        up_grad = (active_grad * gate * sigmoid_gate).astype(BF16)
        gate_up_grads.append(jnp.concatenate([gate_grad, up_grad], axis=1))
        parts.append(dot(gate_up_grads[-1], gate_up_proj, 1, 1))
    norm_grad = scatter_sum(parts)
    grad_down = dot(jnp.concatenate(actives), jnp.concatenate(branch_grads), 0, 0)
    grad_gate_up = dot(jnp.concatenate(normed_second), jnp.concatenate(gate_up_grads), 0, 0)
    unused, norm_pullback = jax.vjp(rms_scaled, middle, gain_second)
    middle_part, gain_second_grad = norm_pullback(norm_grad)
    middle_grad = gradient + middle_part
    branch_grads = gather_rows(middle_grad.astype(BF16))
    mixed_grad = jnp.concatenate([dot(out_proj, rows, 1, 1).astype(BF16) for rows in branch_grads], axis=-1)
    grad_out = dot(mixed, jnp.concatenate(branch_grads), 1, 0)
    query_grad, *piece_grads = flash_backward(
        bounds, queries, pieces, low, high, lse, attended, mixed_grad.reshape(queries.shape), chips
    )
    own_grads = piece_grads[reach * chips :]
    for distance in range(1, reach + 1):
        sent = piece_grads[(reach - distance) * chips : (reach - distance + 1) * chips]
        own_grads = [own + shifted(part, -distance).astype(F32) for own, part in zip(own_grads, sent)]
    qkv_grads, parts = ([], [])
    for index in range(chips):
        cut = slice(index * chip_rows, (index + 1) * chip_rows)
        query_pre = rotary(query_grad[..., cut].reshape(-1, chip_rows), cosine[:, cut], -sine[:, cut])
        key_pre = rotary(own_grads[index][0].reshape(-1, chip_rows), cosine[:, cut], -sine[:, cut])
        joined = jnp.concatenate([query_pre, key_pre, own_grads[index][1]]).astype(BF16)
        joined = joined.reshape(-1, chip_rows)
        qkv_grads.append(joined)
        parts.append(dot(joined, qkv_proj, 0, 1))
    grad_qkv = dot(jnp.concatenate(normed_first), jnp.concatenate(qkv_grads, axis=1), 0, 1)
    norm_grad = scatter_sum(parts)
    unused, first_pullback = jax.vjp(rms_scaled, residual, gain_first)
    residual_part, gain_first_grad = first_pullback(norm_grad)
    weight_grads = (grad_qkv, grad_out, grad_gate_up, grad_down)
    return (middle_grad + residual_part, weight_grads, (gain_first_grad, gain_second_grad))


def shards(
    tokens, cotangent, lengths, gain_attn, w_query, w_key, w_value, w_out, gain_mlp, w_gate, w_up, w_down
):
    rows = tokens.shape[0]
    col, core, half, q = [lax.axis_index(name) for name in ALL]
    group_rows = rows * 2 * lax.axis_size("q")
    group_index = 2 * col + half
    reach = 2 * lax.axis_size("col") // 4
    swap = (2 * q + core) * rows
    inside = jnp.arange(group_rows, dtype=jnp.int32) ^ swap
    token_index = group_index * group_rows + inside
    seq_ends = jnp.cumsum(lengths)
    begun = token_index[:, None] >= seq_ends[None, :]
    seq_begin = jnp.max(jnp.where(begun, seq_ends[None, :], 0), axis=1)
    position = token_index - seq_begin
    first_key = (group_index - reach) * group_rows
    low, high = (seq_begin - first_key, token_index - first_key)
    bounds = jnp.stack(
        [
            jnp.min(low.reshape(-1, BLOCK_Q), axis=1) // BLOCK_K,
            jnp.max(high.reshape(-1, BLOCK_Q), axis=1) // BLOCK_K + 1,
        ],
        axis=1,
    ).reshape(-1)
    bounds = jnp.concatenate([bounds, jnp.stack([swap & (BLOCK_K - 1), swap & -BLOCK_K])])
    frequency = jnp.power(ROPE_BASE, -jnp.arange(HD // 2, dtype=F32) / (HD // 2))
    angles = frequency[:, None] * position.astype(F32)[None, :]
    context = (bounds, low[None, :], high[None, :], jnp.cos(angles), jnp.sin(angles), reach)

    weights = []
    for index in range(LAYERS):
        qkv = jnp.concatenate([w_query[index], w_key[index], w_value[index]], axis=1)
        gate_up = jnp.concatenate([w_gate[index], w_up[index]], axis=1)
        weights.append(
            (
                gain_attn[index],
                fetch_weight(qkv),
                fetch_weight(w_out[index]),
                gain_mlp[index],
                fetch_weight(gate_up),
                fetch_weight(w_down[index]),
            )
        )

    residual = move_tokens(tokens).astype(F32)
    stored = []
    for index in range(LAYERS):
        residual, saved = forward_layer(residual, weights[index], context)
        stored.append(saved)
    output = move_tokens(residual.astype(BF16), back=True).astype(F32)
    gradient = move_tokens(cotangent).astype(F32)
    reduced = [None] * LAYERS
    gains = [None] * LAYERS
    for index in reversed(range(LAYERS)):
        gradient, layer_grads, gains[index] = backward_layer(gradient, weights[index], stored[index], context)
        reduced[index] = [reduce_weight_grad(grad) for grad in layer_grads]
    input_grad = move_tokens(gradient.astype(BF16), back=True).astype(F32)
    gain_first, gain_second = lax.psum(
        (jnp.stack([pair[0] for pair in gains]), jnp.stack([pair[1] for pair in gains])), ALL
    )
    q_width, kv_width = (w_query.shape[2], w_key.shape[2])
    hidden = w_gate.shape[2]
    return (
        output,
        input_grad,
        gain_first,
        jnp.stack([layer[0][:, :q_width] for layer in reduced]),
        jnp.stack([layer[0][:, q_width : q_width + kv_width] for layer in reduced]),
        jnp.stack([layer[0][:, q_width + kv_width :] for layer in reduced]),
        jnp.stack([layer[1] for layer in reduced]),
        gain_second,
        jnp.stack([layer[2][:, :hidden] for layer in reduced]),
        jnp.stack([layer[2][:, hidden:] for layer in reduced]),
        jnp.stack([layer[3] for layer in reduced]),
    )


def solution(mesh):
    wide, narrow = (mesh.shape["wide"], mesh.shape["narrow"])
    split = Mesh(mesh.devices.reshape(wide // 2, 2, 2, narrow // 2), ALL)
    rows, columns, inner = (P(ALL, None), P(None, None, ("half", "q")), P(None, ("half", "q"), None))
    return jax.shard_map(
        shards,
        mesh=split,
        in_specs=(rows, rows, P(), P(), columns, columns, columns, inner, P(), columns, columns, inner),
        out_specs=(rows, rows, P(), columns, columns, columns, inner, P(), columns, columns, inner),
        check_vma=False,
    )
```

```python
import math

import jax
import jax.numpy as jnp
from jax import lax
from jax.experimental import pallas as pl
from jax.experimental.pallas import tpu as pltpu
from jax.sharding import Mesh
from jax.sharding import PartitionSpec as P

HD = 96
LAYERS = 2
EPSILON = 1e-05
ROPE_BASE = 100000.0
MASKED = -1e30
BLOCK_Q = 256
BLOCK_K = 512
SCALE = 1.0 / math.sqrt(HD)
LOG2_SCALE = math.log2(math.e) * SCALE
BF16 = jnp.bfloat16
F32 = jnp.float32

ALL = ("col", "core", "half", "q")


def side_by_side(ref):
    return jnp.concatenate([ref[h] for h in range(ref.shape[0])], axis=-1)


def masked_offsets(bounds_ref, low_ref, high_ref, q_blocks, group):
    low_q = jnp.concatenate([low_ref[...]] * group, axis=-1)
    span_q = jnp.concatenate([high_ref[...]] * group, axis=-1) - low_q
    inner, outer = (bounds_ref[2 * q_blocks], bounds_ref[2 * q_blocks + 1])
    row = lax.broadcasted_iota(jnp.int32, (BLOCK_K, low_q.shape[1]), 0) ^ inner
    return (low_q, span_q, row, outer)


def flash_forward(bounds, queries, pieces, low, high):
    heads, dim, rows = queries.shape
    kv_count, piece_rows = (pieces[0].shape[1], pieces[0].shape[3])
    keys = piece_rows * len(pieces)
    group = heads // kv_count
    q_blocks = rows // BLOCK_Q
    width = group * BLOCK_Q
    count = len(pieces)

    def kernel(bounds_ref, q_ref, low_ref, high_ref, *refs):
        piece_refs = refs[:count]
        out_ref, mixed_ref, lse_ref, k_rows, values = refs[count:]
        i = pl.program_id(1)

        @pl.when(i == 0)
        def _():
            for b in range(count):
                cut = slice(b * piece_rows, (b + 1) * piece_rows)
                k_rows[cut, :] = piece_refs[b][0, 0].T
                values[:, cut] = piece_refs[b][1, 0]

        q = side_by_side(q_ref)
        low_q, span_q, row, outer = masked_offsets(bounds_ref, low_ref, high_ref, q_blocks, group)

        def step(b, carry):
            top, total, accum = carry
            at = pl.multiple_of((b * BLOCK_K) ^ outer, BLOCK_K)
            scores = jnp.dot(k_rows[pl.ds(at, BLOCK_K), :], q, preferred_element_type=F32) * LOG2_SCALE
            offset = row + (b * BLOCK_K - low_q)
            scores = jnp.where((offset >= 0) & (offset <= span_q), scores, MASKED)
            new_top = jnp.maximum(top, jnp.max(scores, axis=0, keepdims=True))
            probs = jnp.exp2(scores - new_top)
            fade = jnp.exp2(top - new_top)
            total = total * fade + jnp.sum(probs, axis=0, keepdims=True)
            accum = accum * fade + jnp.dot(
                values[:, pl.ds(at, BLOCK_K)], probs.astype(BF16), preferred_element_type=F32
            )
            return (new_top, total, accum)

        start = (
            jnp.full((1, width), MASKED, F32),
            jnp.zeros((1, width), F32),
            jnp.zeros((dim, width), F32),
        )
        top, total, accum = lax.fori_loop(bounds_ref[2 * i], bounds_ref[2 * i + 1], step, start)
        out = accum / total
        lse = top + jnp.log2(total)
        for h in range(group):
            cut = slice(h * BLOCK_Q, (h + 1) * BLOCK_Q)
            out_ref[h] = out[:, cut]
            mixed_ref[h] = out[:, cut].astype(BF16)
            lse_ref[h] = lse[:, cut]

    q_spec = pl.BlockSpec((group, dim, BLOCK_Q), lambda j, i, b: (j, 0, i))
    vector = pl.BlockSpec((1, BLOCK_Q), lambda j, i, b: (0, i))
    piece = pl.BlockSpec((2, 1, dim, piece_rows), lambda j, i, b: (0, j, 0, 0))
    return pl.pallas_call(
        kernel,
        grid_spec=pltpu.PrefetchScalarGridSpec(
            num_scalar_prefetch=1,
            grid=(kv_count, q_blocks),
            in_specs=[q_spec, vector, vector] + [piece] * count,
            out_specs=[q_spec, q_spec, pl.BlockSpec((group, 1, BLOCK_Q), lambda j, i, b: (j, 0, i))],
            scratch_shapes=[pltpu.VMEM((keys, dim), BF16), pltpu.VMEM((dim, keys), BF16)],
        ),
        out_shape=[
            jax.ShapeDtypeStruct((heads, dim, rows), F32),
            jax.ShapeDtypeStruct((heads, dim, rows), BF16),
            jax.ShapeDtypeStruct((heads, 1, rows), F32),
        ],
        compiler_params=pltpu.CompilerParams(vmem_limit_bytes=40 << 20),
        cost_estimate=pl.CostEstimate(
            flops=4 * heads * rows * keys * dim, bytes_accessed=6 << 20, transcendentals=heads * rows * keys
        ),
        name="flash_forward",
    )(bounds, queries, low, high, *pieces)


def flash_backward(bounds, queries, pieces, low, high, lse, out, out_grad, own_count):
    heads, dim, rows = queries.shape
    kv_count, piece_rows = (pieces[0].shape[1], pieces[0].shape[3])
    keys = piece_rows * len(pieces)
    group = heads // kv_count
    q_blocks = rows // BLOCK_Q
    width = group * BLOCK_Q
    count = len(pieces)

    def kernel(bounds_ref, q_ref, low_ref, high_ref, lse_ref, out_ref, g_ref, *refs):
        piece_refs = refs[:count]
        dq_ref = refs[count]
        grad_refs = refs[count + 1 : 2 * count + 1]
        k_rows, v_rows, k_lanes, dk_rows, dv_rows = refs[2 * count + 1 :]
        i = pl.program_id(1)

        @pl.when(i == 0)
        def _():
            for b in range(count):
                cut = slice(b * piece_rows, (b + 1) * piece_rows)
                k_rows[cut, :] = piece_refs[b][0, 0].T
                v_rows[cut, :] = piece_refs[b][1, 0].T
                k_lanes[:, cut] = piece_refs[b][0, 0]
            dk_rows[...] = jnp.zeros_like(dk_rows)
            dv_rows[...] = jnp.zeros_like(dv_rows)

        q, g = (side_by_side(q_ref), side_by_side(g_ref))
        q_rows, g_rows = (q.T, g.T)
        delta = jnp.sum(g.astype(F32) * side_by_side(out_ref), axis=0, keepdims=True)
        lse_q = side_by_side(lse_ref)
        low_q, span_q, row, outer = masked_offsets(bounds_ref, low_ref, high_ref, q_blocks, group)

        def step(b, dq):
            cut = pl.ds(pl.multiple_of((b * BLOCK_K) ^ outer, BLOCK_K), BLOCK_K)
            scores = jnp.dot(k_rows[cut, :], q, preferred_element_type=F32) * LOG2_SCALE
            offset = row + (b * BLOCK_K - low_q)
            probs = jnp.exp2(jnp.where((offset >= 0) & (offset <= span_q), scores - lse_q, MASKED))
            prob_grad = jnp.dot(v_rows[cut, :], g, preferred_element_type=F32)
            score_grad = (probs * (prob_grad - delta)).astype(BF16)
            dv_rows[cut, :] += jnp.dot(probs.astype(BF16), g_rows, preferred_element_type=F32)
            dk_rows[cut, :] += jnp.dot(score_grad, q_rows, preferred_element_type=F32)
            return dq + jnp.dot(k_lanes[:, cut], score_grad, preferred_element_type=F32)

        start = jnp.zeros((dim, width), F32)
        dq = lax.fori_loop(bounds_ref[2 * i], bounds_ref[2 * i + 1], step, start) * SCALE
        for h in range(group):
            dq_ref[h] = dq[:, h * BLOCK_Q : (h + 1) * BLOCK_Q]

        @pl.when(i == q_blocks - 1)
        def _():
            for b in range(count):
                cut = slice(b * piece_rows, (b + 1) * piece_rows)
                grad_refs[b][0, 0] = (dk_rows[cut, :].T * SCALE).astype(grad_refs[b].dtype)
                grad_refs[b][1, 0] = dv_rows[cut, :].T.astype(grad_refs[b].dtype)

    q_spec = pl.BlockSpec((group, dim, BLOCK_Q), lambda j, i, b: (j, 0, i))
    vector = pl.BlockSpec((1, BLOCK_Q), lambda j, i, b: (0, i))
    piece = pl.BlockSpec((2, 1, dim, piece_rows), lambda j, i, b: (0, j, 0, 0))
    types = [BF16] * (count - own_count) + [F32] * own_count
    return pl.pallas_call(
        kernel,
        grid_spec=pltpu.PrefetchScalarGridSpec(
            num_scalar_prefetch=1,
            grid=(kv_count, q_blocks),
            in_specs=[q_spec, vector, vector, pl.BlockSpec((group, 1, BLOCK_Q), lambda j, i, b: (j, 0, i))]
            + [q_spec] * 2
            + [piece] * count,
            out_specs=[q_spec] + [piece] * count,
            scratch_shapes=[
                pltpu.VMEM((keys, dim), BF16),
                pltpu.VMEM((keys, dim), BF16),
                pltpu.VMEM((dim, keys), BF16),
                pltpu.VMEM((keys, dim), F32),
                pltpu.VMEM((keys, dim), F32),
            ],
        ),
        out_shape=[jax.ShapeDtypeStruct((heads, dim, rows), F32)]
        + [jax.ShapeDtypeStruct((2, kv_count, dim, piece_rows), t) for t in types],
        compiler_params=pltpu.CompilerParams(vmem_limit_bytes=48 << 20),
        cost_estimate=pl.CostEstimate(
            flops=10 * heads * rows * keys * dim, bytes_accessed=14 << 20, transcendentals=heads * rows * keys
        ),
        name="flash_backward",
    )(bounds, queries, low, high, lse, out, out_grad, *pieces)


def flip_core(block):
    return lax.ppermute(block, "core", [(0, 1), (1, 0)])


def flip_q(block, bit):
    return lax.ppermute(block, "q", [(i, i ^ bit) for i in range(lax.axis_size("q"))])


def q_bits():
    bit, bits = (1, [])
    while bit < lax.axis_size("q"):
        bits.append(bit)
        bit *= 2
    return bits


def gather_rows(own):
    held = [own]
    for bit in q_bits():
        held = held + [flip_q(block, bit) for block in held]
    return [jnp.concatenate([block, flip_core(block)]) for block in held]


def scatter_sum(parts):
    rows = parts[0].shape[0] // 2
    sums = [part[:rows] + flip_core(part[rows:].astype(BF16)).astype(F32) for part in parts]
    for bit in reversed(q_bits()):
        sums = [sums[i] + flip_q(sums[i ^ bit].astype(BF16), bit).astype(F32) for i in range(bit)]
    return sums[0]


def token_route(back):
    q_size = lax.axis_size("q")

    def index(core, half, q):
        return (core * 2 + half) * q_size + q

    pairs = []
    for core in range(2):
        for half in range(2):
            for q in range(q_size):
                rank = 2 * q + core
                pairs.append((index(half, rank // q_size, rank % q_size), index(core, half, q)))
    return [(b, a) for a, b in pairs] if back else pairs


def move_tokens(rows, back=False):
    return lax.ppermute(rows, ("core", "half", "q"), token_route(back))


def shifted(block, distance):
    count = 2 * lax.axis_size("col")
    route = [(i - distance, i) for i in range(count) if 0 <= i - distance < count]
    return lax.ppermute(block, ("col", "half"), route)


class Background:
    def __init__(self):
        self.waiting = []

    def tick(self, main, *jobs):
        due, kept = ([], [])
        for job in jobs:
            due.append((job, next(job)[0]))
        for job, arrays, ticks in self.waiting:
            if ticks > 1:
                kept.append((job, arrays, ticks - 1))
            else:
                due.append((job, arrays))
        self.waiting = kept
        if not due:
            return main
        main, held = lax.optimization_barrier((main, [arrays for unused, arrays in due]))
        for (job, unused), arrays in zip(due, held):
            self.advance(job, arrays)
        return main

    def advance(self, job, arrays):
        try:
            self.waiting.append((job, *job.send(arrays)))
        except StopIteration:
            pass

    def finish(self):
        while self.waiting:
            job, arrays, unused = self.waiting.pop(0)
            self.advance(job, arrays)


def plane_size():
    return 2 * lax.axis_size("col")


def own_piece(weight):
    rows = weight.shape[0] // plane_size()
    at = (lax.axis_index("col") * 2 + lax.axis_index("core")) * rows
    return lax.dynamic_slice_in_dim(weight, at, rows, 0)


def fetch(holder, piece, early=False):
    if not early:
        piece = yield (piece, 0)
    piece = lax.ppermute(piece, "half", [(0, 1), (1, 0)])
    piece = yield (piece, 1)
    holder.append(lax.all_gather(piece, ("col", "core"), axis=0))


def choose(own, other):
    mine = lax.axis_index("core") == lax.axis_index("half")
    return jnp.where(mine, own, other.reshape(own.shape))


def reduce_grad(pack, write, sum_ticks, cross_ticks=1):
    pack = yield (pack, 0)
    part = lax.psum_scatter(pack, "col", scatter_dimension=0, tiled=True)
    part = yield (part, sum_ticks)
    half = lax.axis_index("half")
    part = part.reshape(2, part.shape[0] // 2, part.shape[1])
    kept = lax.dynamic_index_in_dim(part, half, 0, keepdims=False)
    other = lax.dynamic_index_in_dim(part, 1 - half, 0, keepdims=False)
    places = [(core, half) for core in range(2) for half in range(2)]
    kept = lax.ppermute(kept, ("core", "half"), [(c * 2 + h, h * 2 + c) for c, h in places])
    other = lax.ppermute(other, ("core", "half"), [(c * 2 + h, (1 - h) * 2 + c) for c, h in places])
    kept, other = yield ((kept, other), cross_ticks)
    piece = (kept.astype(F32) + other.astype(F32)).astype(BF16)
    if write.gather:
        write(lax.all_gather(piece, ("col", "core"), axis=0))
        return
    count = lax.axis_size("col")
    held = [piece] + [lax.ppermute(piece, "col", [(i, i ^ d) for i in range(count)]) for d in range(1, count)]
    held = yield (held, 1)
    held = jnp.stack(held)
    held, flipped = yield ((held, flip_core(held)), 1)
    write(held, flipped)


def write_grads(held, flipped, targets):
    count = held.shape[0]
    col, core = (lax.axis_index("col"), lax.axis_index("core"))
    order = [(col ^ (i % count)) * 2 + (core ^ (i // count)) for i in range(2 * count)]
    order = jnp.stack(order).astype(jnp.int32)
    old = [target[0] for target in targets if target[0] is not None]

    def kernel(order_ref, held_ref, flipped_ref, *refs):
        outs = refs[len(old) :]

        def write(ref):
            for out, (unused, shape, layer, row, rows, column, columns) in zip(outs, targets):
                out[0] = ref[0, row : row + rows, column : column + columns].astype(F32)

        @pl.when(pl.program_id(0) < count)
        def _():
            write(held_ref)

        @pl.when(pl.program_id(0) >= count)
        def _():
            write(flipped_ref)

    def out_spec(target):
        unused, shape, layer, row, rows, column, columns = target
        return pl.BlockSpec((1, rows, columns), lambda i, order: (layer, order[i], 0))

    aliases, number = ({}, 3)
    for index, target in enumerate(targets):
        if target[0] is not None:
            aliases[number] = index
            number += 1
    block = (1,) + held.shape[1:]
    return pl.pallas_call(
        kernel,
        grid_spec=pltpu.PrefetchScalarGridSpec(
            num_scalar_prefetch=1,
            grid=(2 * count,),
            in_specs=[
                pl.BlockSpec(block, lambda i, order: (jnp.minimum(i, count - 1), 0, 0)),
                pl.BlockSpec(block, lambda i, order: (jnp.maximum(i - count, 0), 0, 0)),
            ]
            + [pl.BlockSpec(memory_space=pl.ANY)] * len(old),
            out_specs=[out_spec(target) for target in targets],
        ),
        out_shape=[jax.ShapeDtypeStruct(target[1], F32) for target in targets],
        input_output_aliases=aliases,
        compiler_params=pltpu.CompilerParams(vmem_limit_bytes=40 << 20),
        cost_estimate=pl.CostEstimate(flops=0, bytes_accessed=3 * 2 * held.size * 2, transcendentals=0),
        name="write_grads",
    )(order, held, flipped, *old)


class Gradients:
    def __init__(self, shapes):
        self.shapes = shapes
        self.arrays = {}

    def job(self, joined, members, sum_ticks, cross_ticks=1):
        plane = plane_size()
        if joined:
            pack = jnp.concatenate([grad.astype(BF16) for *unused, grad in members], axis=1)
        else:
            split = [grad.astype(BF16).reshape(plane, -1, grad.shape[1]) for *unused, grad in members]
            pack = jnp.concatenate(split, axis=1)
            pack = pack.reshape(-1, pack.shape[2])
        row, column, places = (0, 0, [])
        for names, widths, layer, grad in members:
            rows = grad.shape[0] // plane
            for name, width in zip(names, widths):
                places.append((name, layer, row, rows, column, width))
                column += width if joined else 0
            row += 0 if joined else rows

        def write(*pieces):
            if write.gather:
                for name, layer, row, rows, column, width in places:
                    shape = self.shapes[name]
                    array = self.arrays.get(name, jnp.zeros(shape, F32))
                    grad = pieces[0][:, row : row + rows, column : column + width].reshape(shape[1:])
                    self.arrays[name] = array.at[layer].set(grad.astype(F32))
                return
            targets = [(self.arrays.get(name), self.shapes[name], *rest) for name, *rest in places]
            for (name, *unused), array in zip(places, write_grads(*pieces, targets)):
                self.arrays[name] = array

        write.gather = any(place[3] % 16 for place in places)
        return reduce_grad(pack, write, sum_ticks, cross_ticks)


def rms_scaled(residual, gain):
    return residual * lax.rsqrt(jnp.mean(residual * residual, axis=-1, keepdims=True) + EPSILON) * gain


def dot(left, right, left_dim, right_dim):
    return lax.dot_general(left, right, (((left_dim,), (right_dim,)), ((), ())), preferred_element_type=F32)


def rotary(values, cosine, sine):
    values = values.reshape(-1, 2, HD // 2, values.shape[-1])
    first, second = (values[:, 0], values[:, 1])
    turned = jnp.stack([first * cosine - second * sine, second * cosine + first * sine], axis=1)
    return turned.reshape(-1, HD, values.shape[-1])


def forward_layer(residual, weights, context, ticks):
    gain_first, gain_second = weights["gains"]
    bounds, low, high, cosine, sine, reach = context
    q_width, kv_width = weights["widths"]
    residual = ticks("start", residual)
    normed_first = gather_rows(rms_scaled(residual, gain_first).astype(BF16))
    chip_rows = normed_first[0].shape[0]
    query_parts, own_pieces = ([], [])
    for index, rows in enumerate(normed_first):
        cut = slice(index * chip_rows, (index + 1) * chip_rows)
        qkv = dot(weights["qkv"](), rows, 0, 1)
        turned = rotary(qkv[: q_width + kv_width], cosine[:, cut], sine[:, cut]).astype(BF16)
        values = qkv[q_width + kv_width :].astype(BF16).reshape(-1, HD, chip_rows)
        query_parts.append(turned[: q_width // HD])
        own_pieces.append(jnp.stack([turned[q_width // HD :], values]))
    query_parts, own_pieces = ticks("keys", (query_parts, own_pieces))
    pieces = []
    for distance in range(reach, 0, -1):
        pieces += [shifted(piece, distance) for piece in own_pieces]
    pieces += own_pieces
    queries = jnp.concatenate(query_parts, axis=-1)
    attended, mixed, lse = flash_forward(bounds, queries, pieces, low, high)
    mixed = ticks("mixed", mixed.reshape(q_width, -1))
    parts = [
        dot(mixed[:, i * chip_rows : (i + 1) * chip_rows], weights["out"](), 0, 0)
        for i in range(len(normed_first))
    ]
    middle = ticks("middle", residual + scatter_sum(parts))
    normed_second = gather_rows(rms_scaled(middle, gain_second).astype(BF16))
    gates, actives, parts = ([], [], [])
    for rows in normed_second:
        gate = dot(rows, weights["gate"](), 1, 0)
        up = dot(rows, weights["up"](), 1, 0)
        active = (jax.nn.silu(gate) * up).astype(BF16)
        gates.append((gate, up))
        actives.append(active)
        parts.append(dot(active, weights["down"](), 1, 0))
    result = ticks("result", middle + scatter_sum(parts))
    saved = (residual, normed_first, queries, pieces, attended, mixed, lse, middle, normed_second, gates, actives)
    return (result, saved)


def backward_layer(gradient, weights, saved, context, ticks):
    gain_first, gain_second = weights["gains"]
    bounds, low, high, cosine, sine, reach = context
    residual, normed_first, queries, pieces, attended, mixed, lse, middle, normed_second, gates, actives = saved
    chip_rows = normed_first[0].shape[0]
    chips = len(normed_first)
    branch_grads = gather_rows(gradient.astype(BF16))
    gate_grads, up_grads, parts = ([], [], [])
    for rows, (gate, up) in zip(branch_grads, gates):
        active_grad = dot(rows, weights["down"](), 1, 1)
        sigmoid_gate = jax.nn.sigmoid(gate)
        gate_grad = (active_grad * up * sigmoid_gate * (1.0 + gate * (1.0 - sigmoid_gate))).astype(BF16)
        up_grad = (active_grad * gate * sigmoid_gate).astype(BF16)
        gate_grads.append(gate_grad)
        up_grads.append(up_grad)
        parts.append(dot(gate_grad, weights["gate"](), 1, 1) + dot(up_grad, weights["up"](), 1, 1))
    norm_grad = scatter_sum(parts)
    normed_rows = jnp.concatenate(normed_second)
    grad_gate = dot(normed_rows, jnp.concatenate(gate_grads), 0, 0).astype(BF16)
    grad_up = dot(normed_rows, jnp.concatenate(up_grads), 0, 0).astype(BF16)
    norm_grad = ticks("mlp", norm_grad, jnp.concatenate([grad_gate, grad_up], axis=1))
    grad_down = dot(jnp.concatenate(actives), jnp.concatenate(branch_grads), 0, 0).astype(BF16)
    unused, norm_pullback = jax.vjp(rms_scaled, middle, gain_second)
    middle_part, gain_second_grad = norm_pullback(norm_grad)
    middle_grad = gradient + middle_part
    branch_grads = gather_rows(middle_grad.astype(BF16))
    mixed_grad = jnp.concatenate(
        [dot(weights["out"](), rows, 1, 1).astype(BF16) for rows in branch_grads], axis=-1
    )
    grad_out = dot(mixed, jnp.concatenate(branch_grads), 1, 0).astype(BF16)
    mixed_grad = ticks("mixed", mixed_grad, grad_out, grad_down)
    query_grad, *piece_grads = flash_backward(
        bounds, queries, pieces, low, high, lse, attended, mixed_grad.reshape(queries.shape), chips
    )
    own_grads = piece_grads[reach * chips :]
    for distance in range(1, reach + 1):
        sent = piece_grads[(reach - distance) * chips : (reach - distance + 1) * chips]
        own_grads = [own + shifted(part, -distance).astype(F32) for own, part in zip(own_grads, sent)]
    qkv_grads, parts = ([], [])
    for index in range(chips):
        cut = slice(index * chip_rows, (index + 1) * chip_rows)
        query_pre = rotary(query_grad[..., cut].reshape(-1, chip_rows), cosine[:, cut], -sine[:, cut])
        key_pre = rotary(own_grads[index][0].reshape(-1, chip_rows), cosine[:, cut], -sine[:, cut])
        joined = jnp.concatenate([query_pre, key_pre, own_grads[index][1]]).astype(BF16)
        qkv_grads.append(joined.reshape(-1, chip_rows))
    qkv_grads = ticks("keys", qkv_grads)
    parts = [dot(joined, weights["qkv"](), 0, 1) for joined in qkv_grads]
    norm_grad = scatter_sum(parts)
    grad_qkv = dot(jnp.concatenate(normed_first), jnp.concatenate(qkv_grads, axis=1), 0, 1).astype(BF16)
    unused, first_pullback = jax.vjp(rms_scaled, residual, gain_first)
    residual_part, gain_first_grad = first_pullback(norm_grad)
    gradient = ticks("result", middle_grad + residual_part, grad_qkv)
    return (gradient, (gain_first_grad, gain_second_grad))


def sum_everywhere(value):
    value = value + flip_core(value)
    value = value + lax.ppermute(value, "half", [(0, 1), (1, 0)])
    for name in ("q", "col"):
        bit = 1
        while bit < lax.axis_size(name):
            value = value + lax.ppermute(value, name, [(i, i ^ bit) for i in range(lax.axis_size(name))])
            bit *= 2
    return value


def shards(
    tokens, cotangent, lengths, gain_attn, w_query, w_key, w_value, w_out, gain_mlp, w_gate, w_up, w_down
):
    rows = tokens.shape[0]
    col, core, half, q = [lax.axis_index(name) for name in ALL]
    group_rows = rows * 2 * lax.axis_size("q")
    group_index = 2 * col + half
    reach = 2 * lax.axis_size("col") // 4
    swap = (2 * q + core) * rows
    inside = jnp.arange(group_rows, dtype=jnp.int32) ^ swap
    token_index = group_index * group_rows + inside
    seq_ends = jnp.cumsum(lengths)
    begun = token_index[:, None] >= seq_ends[None, :]
    seq_begin = jnp.max(jnp.where(begun, seq_ends[None, :], 0), axis=1)
    position = token_index - seq_begin
    first_key = (group_index - reach) * group_rows
    low, high = (seq_begin - first_key, token_index - first_key)
    bounds = jnp.stack(
        [
            jnp.min(low.reshape(-1, BLOCK_Q), axis=1) // BLOCK_K,
            jnp.max(high.reshape(-1, BLOCK_Q), axis=1) // BLOCK_K + 1,
        ],
        axis=1,
    ).reshape(-1)
    bounds = jnp.concatenate([bounds, jnp.stack([swap & (BLOCK_K - 1), swap & -BLOCK_K])])
    frequency = jnp.power(ROPE_BASE, -jnp.arange(HD // 2, dtype=F32) / (HD // 2))
    angles = frequency[:, None] * position.astype(F32)[None, :]
    context = (bounds, low[None, :], high[None, :], jnp.cos(angles), jnp.sin(angles), reach)

    q_width, kv_width, hidden = (w_query.shape[2], w_key.shape[2], w_gate.shape[2])
    background = Background()

    def layer_weights(index):
        cache, attn, mlp = ({}, [], [])
        qkv = jnp.concatenate([w_query[index], w_key[index], w_value[index]], axis=1)
        qkv_piece = own_piece(qkv)
        rows, width = qkv_piece.shape

        def once(name, make):
            def get():
                if name not in cache:
                    cache[name] = make()
                return cache[name]

            return get

        attn_piece = jnp.concatenate([qkv_piece, own_piece(w_out[index]).reshape(-1, width)])
        mlp_piece = jnp.concatenate(
            [own_piece(w_gate[index]), own_piece(w_up[index]), own_piece(w_down[index]).reshape(rows, hidden)]
        )
        weights = {
            "gains": (gain_attn[index], gain_mlp[index]),
            "widths": (q_width, kv_width),
            "qkv": once("qkv", lambda: choose(qkv, attn[0][:, :rows])),
            "out": once("out", lambda: choose(w_out[index], attn[0][:, rows:])),
            "gate": once("gate", lambda: choose(w_gate[index], mlp[0][:, :rows])),
            "up": once("up", lambda: choose(w_up[index], mlp[0][:, rows : 2 * rows])),
            "down": once("down", lambda: choose(w_down[index], mlp[0][:, 2 * rows :])),
        }
        return (weights, lambda early=False: fetch(attn, attn_piece, early), lambda: fetch(mlp, mlp_piece))

    layers = [layer_weights(index) for index in range(LAYERS)]

    def forward_ticks(index):
        def ticks(name, main):
            jobs = []
            if name == "start" and index == 0:
                jobs = [layers[0][2]()]
            if name == "mixed" and index + 1 < LAYERS:
                jobs = [layers[index + 1][1]()]
            if name == "middle" and index + 1 < LAYERS:
                jobs = [layers[index + 1][2]()]
            return background.tick(main, *jobs)

        return ticks

    first = layers[0][1](early=True)
    background.waiting.append((first, *next(first)))
    residual = move_tokens(tokens).astype(F32)
    stored = []
    for index in range(LAYERS):
        residual, saved = forward_layer(residual, layers[index][0], context, forward_ticks(index))
        stored.append(saved)
    cotangent = lax.optimization_barrier((cotangent, stored[0][7]))[0]
    gradient = move_tokens(cotangent).astype(F32)
    output = move_tokens(residual.astype(BF16), back=True).astype(F32)
    names = ("query", "key", "value", "out", "gate", "up", "down")
    shapes = [w.shape for w in (w_query, w_key, w_value, w_out, w_gate, w_up, w_down)]
    grads = Gradients(dict(zip(names, shapes)))

    def backward_ticks(index):
        def ticks(name, main, *new):
            jobs = []
            if name == "mlp":
                jobs = [grads.job(1, [(names[4:6], (hidden, hidden), index, new[0])], 2)]
            if name == "mixed":
                members = [
                    (names[3:4], w_out.shape[2:], index, new[0]),
                    (names[6:], w_down.shape[2:], index, new[1]),
                ]
                jobs = [grads.job(0, members, 3)]
            if name == "result":
                jobs = [grads.job(1, [(names[:3], (q_width, kv_width, kv_width), index, new[0])], 1, 2)]
            return background.tick(main, *jobs)

        return ticks

    gains = [None] * LAYERS
    for index in reversed(range(LAYERS)):
        gradient, gains[index] = backward_layer(
            gradient, layers[index][0], stored[index], context, backward_ticks(index)
        )
    input_grad = move_tokens(gradient.astype(BF16), back=True).astype(F32)
    gain_grads = sum_everywhere(jnp.stack([pair[0] for pair in gains] + [pair[1] for pair in gains]))
    background.finish()
    array = grads.arrays
    return (
        output,
        input_grad,
        gain_grads[:LAYERS],
        array["query"],
        array["key"],
        array["value"],
        array["out"],
        gain_grads[LAYERS:],
        array["gate"],
        array["up"],
        array["down"],
    )


def solution(mesh):
    wide, narrow = (mesh.shape["wide"], mesh.shape["narrow"])
    split = Mesh(mesh.devices.reshape(wide // 2, 2, 2, narrow // 2), ALL)
    rows, columns, inner = (P(ALL, None), P(None, None, ("half", "q")), P(None, ("half", "q"), None))
    return jax.shard_map(
        shards,
        mesh=split,
        in_specs=(rows, rows, P(), P(), columns, columns, columns, inner, P(), columns, columns, inner),
        out_specs=(rows, rows, P(), columns, columns, columns, inner, P(), columns, columns, inner),
        check_vma=False,
    )
```
